768 devices in a mesh: blk: 96 (over x, y, z_lo), uly: 8 (over z_hi, core).
Axes of the slice: x: 4, y: 8, z: 12 (z_hi: 4, z_lo: 3; z = z_hi * 3 + z_lo), core: 2. Of those that a mesh axis runs over, the one named last changes fastest.
Arguments:
- stored_query_rows: bfloat16 [12288, 5120], P('blk', 'uly'), may hold values from -4 to 4
- key_states: bfloat16 [12288, 1024], P('blk', 'uly'), may hold values from -4 to 4
- value_states: bfloat16 [12288, 1024], P('blk', 'uly'), may hold values from -6 to 6
- attn_output: bfloat16 [12288, 5120], P('blk', 'uly'), may hold values from -6 to 6
- output_grad: bfloat16 [12288, 5120], P(('blk', 'uly')), may hold values from -48 to 48
- logsumexp: float32 [40, 12288], P('uly', 'blk'), may hold values from 7 to 8.5
Outputs:
- query_gradient: bfloat16 [12288, 5120], P(('blk', 'uly'))
- key_grad: bfloat16 [12288, 1024], P(('blk', 'uly'))
- value_grad: bfloat16 [12288, 1024], P(('blk', 'uly'))
The draws below stay inside these ranges and needn't reach their ends.
All inputs are finite; a program needn't handle non-finite values.
Results may differ from the reference program's by a relative error of at most 0.0055.
Values may be sent and summed in bfloat16 or wider, within the bound.
A program may use at most 32 MiB of HBM per device.

```python
import jax
import jax.numpy as jnp
from jax import lax

QHEADS = 40
KVHEADS = 8
HEAD_DIM = 128
STEPS = 3
BLK = 128
BLOCKS = 96
SEQ = 12288


def block_levels(rng, dims, cuts, low, top_value):
    loudness = 1.0
    for position, parts in cuts:
        steps = jax.random.uniform(jax.random.fold_in(jax.random.fold_in(rng, 6), position), (parts,), jnp.float32, low / len(cuts), top_value / len(cuts))
        loudness = loudness * jnp.repeat(jnp.exp(steps), dims[position] // parts).reshape((-1,) + (1,) * (len(dims) - 1 - position))
    return loudness


def gaussian(rng, shape, spread, bound, pieces=(), kind=jnp.bfloat16):
    array = spread * jax.random.normal(rng, shape, jnp.float32)
    if pieces:
        array = array * block_levels(rng, shape, pieces, -0.22, 0.18)
    return jnp.clip(array, -bound, bound).astype(kind)


def setup_inputs(seed: int = 0) -> dict:
    keys = jax.random.split(jax.random.key(seed), 7)
    return {
        "stored_query_rows": gaussian(keys[0], (SEQ, QHEADS * HEAD_DIM), 1.0, 4.0, ((0, 96), (1, 8))),
        "key_states": gaussian(keys[1], (SEQ, KVHEADS * HEAD_DIM), 1.0, 4.0, ((0, 96), (1, 8))),
        "value_states": gaussian(keys[2], (SEQ, KVHEADS * HEAD_DIM), 1.0, 6.0, ((0, 96), (1, 8))),
        "attn_output": gaussian(keys[3], (SEQ, QHEADS * HEAD_DIM), 1.0, 6.0, ((0, 96), (1, 8))),
        "output_grad": gaussian(keys[4], (SEQ, QHEADS * HEAD_DIM), 8.0, 48.0, ((0, 768),)),
        "logsumexp": jnp.clip(7.0 + 1.5 * jax.random.uniform(keys[5], (QHEADS, SEQ), jnp.float32) ** block_levels(keys[5], (QHEADS, SEQ), ((0, 8), (1, 96)), -0.2, 0.2), 7.0, 8.5),
    }


def block_grads(query_heads, gradient_per_head, lse_heads, delta_per_head, key_block, value_block, score_scale):
    query_wide = query_heads.astype(jnp.float32)
    gradient_side_by_side = gradient_per_head.astype(jnp.float32)
    key_wide = key_block.astype(jnp.float32)
    value_wide = value_block.astype(jnp.float32)
    scores = jnp.einsum("tgrd,ugd->grtu", query_wide, key_wide)
    prob_tile = jnp.exp(scores * score_scale - lse_heads[..., None])
    grad_probs = jnp.einsum("tgrd,ugd->grtu", gradient_side_by_side, value_wide)
    grad_scores = (prob_tile * (grad_probs - delta_per_head[..., None])).astype(jnp.bfloat16).astype(jnp.float32)
    prob_low = prob_tile.astype(jnp.bfloat16).astype(jnp.float32)
    value_part = jnp.einsum("grtu,tgrd->ugd", prob_low, gradient_side_by_side)
    query_part = jnp.einsum("grtu,ugd->tgrd", grad_scores, key_wide)
    key_portion = jnp.einsum("grtu,tgrd->ugd", grad_scores, query_wide)
    return query_part, key_portion, value_part


def reference(stored_query_rows, key_states, value_states, attn_output, output_grad, logsumexp):
    group_size = QHEADS // KVHEADS
    score_scale = HEAD_DIM ** -0.5
    query_blocks = stored_query_rows.reshape(BLOCKS, BLK, KVHEADS, group_size, HEAD_DIM)
    grad_blocks = output_grad.reshape(BLOCKS, BLK, KVHEADS, group_size, HEAD_DIM)
    out_blocks = attn_output.reshape(BLOCKS, BLK, KVHEADS, group_size, HEAD_DIM)
    key_blocks = key_states.reshape(BLOCKS, BLK, KVHEADS, HEAD_DIM)
    value_blocks = value_states.reshape(BLOCKS, BLK, KVHEADS, HEAD_DIM)
    lse_blocks = logsumexp.reshape(KVHEADS, group_size, BLOCKS, BLK).transpose(2, 0, 1, 3)

    def one_block(index):
        query_heads = query_blocks[index]
        gradient_per_head = grad_blocks[index]
        output_per_head = out_blocks[index]
        lse_heads = lse_blocks[index]
        delta_per_head = jnp.einsum("lpnc,lpnc->pnl", gradient_per_head.astype(jnp.float32), output_per_head.astype(jnp.float32))
        query_sum = jnp.zeros((BLK, KVHEADS, group_size, HEAD_DIM), jnp.float32)
        key_list = []
        value_list = []
        for offset in range(STEPS):
            source = ((index - offset) % BLOCKS).astype(jnp.int32)
            query_part, key_portion, value_part = block_grads(query_heads, gradient_per_head, lse_heads, delta_per_head,
                                                           key_blocks[source], value_blocks[source], score_scale)
            query_sum = query_sum + query_part
            key_list.append(key_portion)
            value_list.append(value_part)
        query_low = (score_scale * query_sum).astype(jnp.bfloat16)
        return query_low, jnp.stack(key_list), jnp.stack(value_list)

    query_low, key_parts, value_parts = lax.map(one_block, jnp.arange(BLOCKS, dtype=jnp.int32))
    key_total = jnp.zeros((BLOCKS, BLK, KVHEADS, HEAD_DIM), jnp.float32)
    value_total = jnp.zeros((BLOCKS, BLK, KVHEADS, HEAD_DIM), jnp.float32)
    for offset in range(STEPS):
        key_total = key_total + jnp.roll(key_parts[:, offset], -offset, axis=0)
        value_total = value_total + jnp.roll(value_parts[:, offset], -offset, axis=0)
    query_gradient = query_low.reshape(SEQ, QHEADS * HEAD_DIM)
    key_grad = (score_scale * key_total).astype(jnp.bfloat16).reshape(SEQ, KVHEADS * HEAD_DIM)
    value_grad = value_total.astype(jnp.bfloat16).reshape(SEQ, KVHEADS * HEAD_DIM)
    return query_gradient, key_grad, value_grad
```

```python
import jax
import jax.numpy as jnp
from jax import lax
from jax.experimental import pallas as pl
from jax.experimental.pallas import tpu as pltpu
from jax.sharding import PartitionSpec as P

QHEADS = 40
KVHEADS = 8
HEAD_DIM = 128
STEPS = 3
MESH = pl.DeviceIdType.MESH
F32 = jnp.float32
BF16 = jnp.bfloat16

HOPS = ((2, 0), (2, 1), (1, 0), (3, 0), (1, 1), (3, 1), (0, 1))


def dot_nt(a, b):
    return lax.dot_general(a, b, (((1,), (1,)), ((), ())), preferred_element_type=F32)


def dot_nn(a, b):
    return lax.dot_general(a, b, (((1,), (0,)), ((), ())), preferred_element_type=F32)


def kernel(
    blocks, ulys,
    q_hbm, k_hbm, v_hbm, o_hbm, g_hbm, lse_hbm,
    dq_out, dk_out, dv_out,
    q, k, v, o, g, lse, kt, prob, prob_low, dscore, delta, own, part, far, dq, final,
    local_sem, local_out_sem, g_send, g_recv, kv_send, kv_recv, p_send, p_recv,
    dq_send, dq_recv, f_send, f_recv,
):
    group = q.shape[1] // HEAD_DIM
    tokens = q.shape[0]
    piece = tokens // ulys
    width = q.shape[1]
    scale = HEAD_DIM ** -0.5
    b = lax.axis_index("blk")
    u = lax.axis_index("uly")
    chips = ulys // 2
    zc = u // 2
    core = u % 2

    def peer(hop):
        return ((zc + hop[0]) % chips) * 2 + (core + hop[1]) % 2

    peers = [peer(hop) for hop in HOPS]
    later = [(b + i) % blocks for i in range(STEPS)]
    earlier = [(b + blocks - i) % blocks for i in range(STEPS)]

    barrier = pltpu.get_barrier_semaphore()
    for p in peers:
        pl.semaphore_signal(barrier, inc=1, device_id=(b, p), device_id_type=MESH)
    for i in range(1, STEPS):
        pl.semaphore_signal(barrier, inc=1, device_id=(later[i], u), device_id_type=MESH)
        pl.semaphore_signal(barrier, inc=1, device_id=(earlier[i], u), device_id_type=MESH)

    def cols(index, size):
        return pl.ds(pl.multiple_of(index * size, size), size)

    locals_ = [
        pltpu.make_async_copy(q_hbm, q, local_sem.at[0]),
        pltpu.make_async_copy(k_hbm, k.at[0], local_sem.at[1]),
        pltpu.make_async_copy(lse_hbm, lse, local_sem.at[2]),
        pltpu.make_async_copy(v_hbm, v.at[0], local_sem.at[3]),
        pltpu.make_async_copy(o_hbm, o, local_sem.at[4]),
        pltpu.make_async_copy(g_hbm.at[:, cols(u, width)], g.at[cols(u, piece), :], local_sem.at[5]),
    ]
    for c in locals_:
        c.start()
    pl.semaphore_wait(barrier, len(peers) + 2 * (STEPS - 1))

    def remote(src, dst, send, recv, to):
        return pltpu.make_async_remote_copy(
            src_ref=src, dst_ref=dst, send_sem=send, recv_sem=recv, device_id=to, device_id_type=MESH
        )

    g_copies = [
        remote(g_hbm.at[:, cols(p, width)], g.at[cols(u, piece), :], g_send.at[n], g_recv.at[n], (b, p))
        for n, p in enumerate(peers)
    ]
    kv_copies = []
    for i in range(1, STEPS):
        kv_copies.append(remote(k_hbm, k.at[i], kv_send.at[0, i - 1], kv_recv.at[0, i - 1], (later[i], u)))
        kv_copies.append(remote(v_hbm, v.at[i], kv_send.at[1, i - 1], kv_recv.at[1, i - 1], (later[i], u)))
    for c in g_copies[:2]:
        c.start()
    for c in kv_copies[0::2]:
        c.start()
    for c in g_copies[2:]:
        c.start()
    for c in kv_copies[1::2]:
        c.start()

    def head(r):
        return slice(r * HEAD_DIM, (r + 1) * HEAD_DIM)

    for c in locals_[:3]:
        c.wait()
    for i in range(STEPS):
        if i:
            kv_copies[2 * (i - 1)].wait_recv()
        keys = k[i]
        kt[:, head(i)] = keys.T
        for r in range(group):
            s = dot_nt(keys, q[:, head(r)])
            p = jnp.exp(s * scale - lse[r : r + 1, :])
            prob[i, :, head(r)] = p
            prob_low[i, :, head(r)] = p.astype(BF16)

    for c in locals_[3:]:
        c.wait()
    for c in g_copies:
        c.wait_recv()

    grads = jnp.concatenate([g[:, head(r)] for r in range(group)], axis=0)
    queries = jnp.concatenate([q[:, head(r)] for r in range(group)], axis=0)
    part_copies = []

    def send_part(kind, i):
        c = remote(
            part.at[kind, i - 1], far.at[kind, i - 1], p_send.at[kind, i - 1], p_recv.at[kind, i - 1],
            (earlier[i], u),
        )
        c.start()
        part_copies.append(c)

    for i in (2, 1, 0):
        dv = dot_nn(prob_low[i], grads)
        if i:
            part[1, i - 1] = dv.astype(BF16)
            send_part(1, i)
        else:
            own[1] = dv

    ones = jnp.ones((8, HEAD_DIM), BF16)
    for r in range(group):
        product = g[:, head(r)].astype(F32) * o[:, head(r)].astype(F32)
        high = product.astype(BF16)
        low = (product - high.astype(F32)).astype(BF16)
        delta[:, head(r)] = dot_nt(ones, high) + dot_nt(ones, low)

    for c in kv_copies[1::2]:
        c.wait_recv()
    for i in (2, 1, 0):
        for r in range(group):
            dp = dot_nt(v[i], g[:, head(r)])
            ds = prob[i, :, head(r)] * (dp - delta[0:1, head(r)])
            dscore[head(i), head(r)] = ds.astype(BF16)
        dk = dot_nn(dscore[head(i), :], queries)
        if i:
            part[0, i - 1] = dk.astype(BF16)
            send_part(0, i)
        else:
            own[0] = dk

    for r in range(group):
        dqt = dot_nn(kt[...], dscore[:, head(r)])
        dq[:, head(r)] = (dqt.T * scale).astype(BF16)

    dq_copies = []
    for n, p in enumerate(peers):
        c = remote(dq.at[cols(p, piece), :], dq_out.at[:, cols(u, width)], dq_send.at[n], dq_recv.at[n], (b, p))
        c.start()
        dq_copies.append(c)
    keep = [pltpu.make_async_copy(dq.at[cols(u, piece), :], dq_out.at[:, cols(u, width)], local_out_sem.at[0])]
    keep[0].start()

    for c in part_copies:
        c.wait_recv()
    final_copies = []
    for kind, out, factor in ((1, dv_out, None), (0, dk_out, scale)):
        total = own[kind] + far[kind, 0].astype(F32) + far[kind, 1].astype(F32)
        if factor is not None:
            total = total * factor
        final[kind] = total.astype(BF16)
        for n, p in enumerate(peers):
            c = remote(
                final.at[kind, cols(p, piece), :], out.at[:, cols(u, HEAD_DIM)],
                f_send.at[kind, n], f_recv.at[kind, n], (b, p),
            )
            c.start()
            final_copies.append(c)
        c = pltpu.make_async_copy(
            final.at[kind, cols(u, piece), :], out.at[:, cols(u, HEAD_DIM)], local_out_sem.at[1 + kind]
        )
        c.start()
        keep.append(c)

    for c in g_copies + kv_copies + part_copies:
        c.wait_send()
    for c in keep:
        c.wait()
    for c in dq_copies + final_copies:
        c.wait()


def solution(mesh):
    blocks = mesh.shape["blk"]
    ulys = mesh.shape["uly"]

    def body(q, k, v, o, g, lse):
        tokens, width = q.shape
        group = width // HEAD_DIM
        piece = tokens // ulys
        peers = len(HOPS)
        far = STEPS - 1
        dma = pltpu.SemaphoreType.DMA
        return pl.pallas_call(
            lambda *refs: kernel(blocks, ulys, *refs),
            out_shape=(
                jax.ShapeDtypeStruct((piece, width * ulys), BF16),
                jax.ShapeDtypeStruct((piece, HEAD_DIM * ulys), BF16),
                jax.ShapeDtypeStruct((piece, HEAD_DIM * ulys), BF16),
            ),
            in_specs=[pl.BlockSpec(memory_space=pl.ANY)] * 6,
            out_specs=(pl.BlockSpec(memory_space=pl.ANY),) * 3,
            scratch_shapes=[
                pltpu.VMEM((tokens, width), BF16),
                pltpu.VMEM((STEPS, tokens, HEAD_DIM), BF16),
                pltpu.VMEM((STEPS, tokens, HEAD_DIM), BF16),
                pltpu.VMEM((tokens, width), BF16),
                pltpu.VMEM((tokens, width), BF16),
                pltpu.VMEM((group, tokens), F32),
                pltpu.VMEM((HEAD_DIM, STEPS * tokens), BF16),
                pltpu.VMEM((STEPS, tokens, width), F32),
                pltpu.VMEM((STEPS, tokens, width), BF16),
                pltpu.VMEM((STEPS * tokens, width), BF16),
                pltpu.VMEM((8, width), F32),
                pltpu.VMEM((2, tokens, HEAD_DIM), F32),
                pltpu.VMEM((2, far, tokens, HEAD_DIM), BF16),
                pltpu.VMEM((2, far, tokens, HEAD_DIM), BF16),
                pltpu.VMEM((tokens, width), BF16),
                pltpu.VMEM((2, tokens, HEAD_DIM), BF16),
                dma((6,)),
                dma((3,)),
                dma((peers,)),
                dma((peers,)),
                dma((2, far)),
                dma((2, far)),
                dma((2, far)),
                dma((2, far)),
                dma((peers,)),
                dma((peers,)),
                dma((2, peers)),
                dma((2, peers)),
            ],
            compiler_params=pltpu.CompilerParams(collective_id=0, has_side_effects=True),
            name="grads",
        )(q, k, v, o, g, lse)

    placed = (
        P("blk", "uly"),
        P("blk", "uly"),
        P("blk", "uly"),
        P("blk", "uly"),
        P(("blk", "uly"), None),
        P("uly", "blk"),
    )
    return jax.shard_map(
        body,
        mesh=mesh,
        in_specs=placed,
        out_specs=(P(("blk", "uly"), None), P(("blk", "uly"), None), P(("blk", "uly"), None)),
        check_vma=False,
    )
```

```python
import jax
import jax.numpy as jnp
from jax import lax
from jax.experimental import pallas as pl
from jax.experimental.pallas import tpu as pltpu
from jax.sharding import PartitionSpec as P

QHEADS = 40
KVHEADS = 8
HEAD_DIM = 128
STEPS = 3
MESH = pl.DeviceIdType.MESH
F32 = jnp.float32
BF16 = jnp.bfloat16

HOPS = ((2, 0), (2, 1), (1, 0), (3, 0), (1, 1), (3, 1), (0, 1))


def dot_nt(a, b):
    return lax.dot_general(a, b, (((1,), (1,)), ((), ())), preferred_element_type=F32)


def dot_nn(a, b):
    return lax.dot_general(a, b, (((1,), (0,)), ((), ())), preferred_element_type=F32)


def kernel(
    blocks, ulys,
    q_hbm, k_hbm, v_hbm, o_hbm, g_hbm, lse_hbm,
    dq_out, dk_out, dv_out,
    q, k, v, o, g, lse, kt, prob, prob_low, dscore, delta, own, part, far, dq, final,
    local_sem, local_out_sem, g_send, g_recv, kv_send, kv_recv, p_send, p_recv,
    dq_send, dq_recv, f_send, f_recv,
):
    group = q.shape[1] // HEAD_DIM
    tokens = q.shape[0]
    piece = tokens // ulys
    width = q.shape[1]
    scale = HEAD_DIM ** -0.5
    b = lax.axis_index("blk")
    u = lax.axis_index("uly")
    chips = ulys // 2
    zc = u // 2
    core = u % 2

    def peer(hop):
        return ((zc + hop[0]) % chips) * 2 + (core + hop[1]) % 2

    peers = [peer(hop) for hop in HOPS]
    later = [(b + i) % blocks for i in range(STEPS)]
    earlier = [(b + blocks - i) % blocks for i in range(STEPS)]

    barrier = pltpu.get_barrier_semaphore()
    for p in peers:
        pl.semaphore_signal(barrier, inc=1, device_id=(b, p), device_id_type=MESH)
    for i in range(1, STEPS):
        pl.semaphore_signal(barrier, inc=1, device_id=(later[i], u), device_id_type=MESH)
        pl.semaphore_signal(barrier, inc=1, device_id=(earlier[i], u), device_id_type=MESH)

    def cols(index, size):
        return pl.ds(pl.multiple_of(index * size, size), size)

    locals_ = [
        pltpu.make_async_copy(q_hbm, q, local_sem.at[0]),
        pltpu.make_async_copy(k_hbm, k.at[0], local_sem.at[1]),
        pltpu.make_async_copy(lse_hbm, lse, local_sem.at[2]),
        pltpu.make_async_copy(v_hbm, v.at[0], local_sem.at[3]),
        pltpu.make_async_copy(o_hbm, o, local_sem.at[4]),
        pltpu.make_async_copy(g_hbm.at[:, cols(u, width)], g.at[cols(u, piece), :], local_sem.at[5]),
    ]
    for c in locals_:
        c.start()
    pl.semaphore_wait(barrier, len(peers) + 2 * (STEPS - 1))

    def remote(src, dst, send, recv, to):
        return pltpu.make_async_remote_copy(
            src_ref=src, dst_ref=dst, send_sem=send, recv_sem=recv, device_id=to, device_id_type=MESH
        )

    g_copies = [
        remote(g_hbm.at[:, cols(p, width)], g.at[cols(u, piece), :], g_send.at[n], g_recv.at[n], (b, p))
        for n, p in enumerate(peers)
    ]
    kv_copies = []
    for i in range(1, STEPS):
        kv_copies.append(remote(k_hbm, k.at[i], kv_send.at[0, i - 1], kv_recv.at[0, i - 1], (later[i], u)))
        kv_copies.append(remote(v_hbm, v.at[i], kv_send.at[1, i - 1], kv_recv.at[1, i - 1], (later[i], u)))
    for c in g_copies[:2]:
        c.start()
    for c in kv_copies[0::2]:
        c.start()
    for c in g_copies[2:]:
        c.start()
    for c in kv_copies[1::2]:
        c.start()

    def head(r):
        return slice(r * HEAD_DIM, (r + 1) * HEAD_DIM)

    for c in locals_[:3]:
        c.wait()
    for i in range(STEPS):
        if i:
            kv_copies[2 * (i - 1)].wait_recv()
        keys = k[i]
        kt[:, head(i)] = keys.T
        for r in range(group):
            s = dot_nt(keys, q[:, head(r)])
            p = jnp.exp(s * scale - lse[r : r + 1, :])
            prob[i, :, head(r)] = p
            prob_low[i, :, head(r)] = p.astype(BF16)

    for c in locals_[3:]:
        c.wait()
    for c in g_copies:
        c.wait_recv()

    grads = jnp.concatenate([g[:, head(r)] for r in range(group)], axis=0)
    queries = jnp.concatenate([q[:, head(r)] for r in range(group)], axis=0)
    part_copies = []

    def send_part(kind, i):
        c = remote(
            part.at[kind, i - 1], far.at[kind, i - 1], p_send.at[kind, i - 1], p_recv.at[kind, i - 1],
            (earlier[i], u),
        )
        c.start()
        part_copies.append(c)

    for i in (2, 1, 0):
        dv = dot_nn(prob_low[i], grads)
        if i:
            part[1, i - 1] = dv.astype(BF16)
            send_part(1, i)
        else:
            own[1] = dv

    ones = jnp.ones((8, HEAD_DIM), BF16)
    for r in range(group):
        product = g[:, head(r)].astype(F32) * o[:, head(r)].astype(F32)
        high = product.astype(BF16)
        low = (product - high.astype(F32)).astype(BF16)
        delta[:, head(r)] = dot_nt(ones, high) + dot_nt(ones, low)

    for c in kv_copies[1::2]:
        c.wait_recv()
    for i in (2, 1, 0):
        for r in range(group):
            dp = dot_nt(v[i], g[:, head(r)])
            ds = prob[i, :, head(r)] * (dp - delta[0:1, head(r)])
            dscore[head(i), head(r)] = ds.astype(BF16)
        dk = dot_nn(dscore[head(i), :], queries)
        if i:
            part[0, i - 1] = dk.astype(BF16)
            send_part(0, i)
        else:
            own[0] = dk

    for r in range(group):
        dqt = dot_nn(kt[...], dscore[:, head(r)])
        dq[:, head(r)] = (dqt.T * scale).astype(BF16)

    dq_copies = []
    for n, p in enumerate(peers):
        c = remote(dq.at[cols(p, piece), :], dq_out.at[:, cols(u, width)], dq_send.at[n], dq_recv.at[n], (b, p))
        c.start()
        dq_copies.append(c)
    keep = [pltpu.make_async_copy(dq.at[cols(u, piece), :], dq_out.at[:, cols(u, width)], local_out_sem.at[0])]
    keep[0].start()

    for c in part_copies:
        c.wait_recv()
    final_copies = []
    for kind, out, factor in ((1, dv_out, None), (0, dk_out, scale)):
        total = own[kind] + far[kind, 0].astype(F32) + far[kind, 1].astype(F32)
        if factor is not None:
            total = total * factor
        final[kind] = total.astype(BF16)
        for n, p in enumerate(peers):
            c = remote(
                final.at[kind, cols(p, piece), :], out.at[:, cols(u, HEAD_DIM)],
                f_send.at[kind, n], f_recv.at[kind, n], (b, p),
            )
            c.start()
            final_copies.append(c)
        c = pltpu.make_async_copy(
            final.at[kind, cols(u, piece), :], out.at[:, cols(u, HEAD_DIM)], local_out_sem.at[1 + kind]
        )
        c.start()
        keep.append(c)

    for c in g_copies + kv_copies + part_copies:
        c.wait_send()
    for c in keep:
        c.wait()
    for c in dq_copies + final_copies:
        c.wait()


def put_out(a, b, c, a_out, b_out, c_out, sem):
    copies = [
        pltpu.make_async_copy(src, dst, sem.at[n])
        for n, (src, dst) in enumerate(((a, a_out), (b, b_out), (c, c_out)))
    ]
    for copy in copies:
        copy.start()
    for copy in copies:
        copy.wait()


def solution(mesh):
    blocks = mesh.shape["blk"]
    ulys = mesh.shape["uly"]

    def body(q, k, v, o, g, lse):
        tokens, width = q.shape
        group = width // HEAD_DIM
        piece = tokens // ulys
        peers = len(HOPS)
        far = STEPS - 1
        dma = pltpu.SemaphoreType.DMA
        held = pl.pallas_call(
            lambda *refs: kernel(blocks, ulys, *refs),
            out_shape=(
                pltpu.VMEM((piece, width * ulys), BF16),
                pltpu.VMEM((piece, HEAD_DIM * ulys), BF16),
                pltpu.VMEM((piece, HEAD_DIM * ulys), BF16),
            ),
            in_specs=[pl.BlockSpec(memory_space=pl.ANY)] * 6,
            out_specs=(pl.BlockSpec(memory_space=pl.ANY),) * 3,
            scratch_shapes=[
                pltpu.VMEM((tokens, width), BF16),
                pltpu.VMEM((STEPS, tokens, HEAD_DIM), BF16),
                pltpu.VMEM((STEPS, tokens, HEAD_DIM), BF16),
                pltpu.VMEM((tokens, width), BF16),
                pltpu.VMEM((tokens, width), BF16),
                pltpu.VMEM((group, tokens), F32),
                pltpu.VMEM((HEAD_DIM, STEPS * tokens), BF16),
                pltpu.VMEM((STEPS, tokens, width), F32),
                pltpu.VMEM((STEPS, tokens, width), BF16),
                pltpu.VMEM((STEPS * tokens, width), BF16),
                pltpu.VMEM((8, width), F32),
                pltpu.VMEM((2, tokens, HEAD_DIM), F32),
                pltpu.VMEM((2, far, tokens, HEAD_DIM), BF16),
                pltpu.VMEM((2, far, tokens, HEAD_DIM), BF16),
                pltpu.VMEM((tokens, width), BF16),
                pltpu.VMEM((2, tokens, HEAD_DIM), BF16),
                dma((6,)),
                dma((3,)),
                dma((peers,)),
                dma((peers,)),
                dma((2, far)),
                dma((2, far)),
                dma((2, far)),
                dma((2, far)),
                dma((peers,)),
                dma((peers,)),
                dma((2, peers)),
                dma((2, peers)),
            ],
            compiler_params=pltpu.CompilerParams(collective_id=0, has_side_effects=True),
            name="grads",
        )(q, k, v, o, g, lse)
        return pl.pallas_call(
            put_out,
            out_shape=tuple(jax.ShapeDtypeStruct(x.shape, x.dtype) for x in held),
            in_specs=[pl.BlockSpec(memory_space=pl.ANY)] * 3,
            out_specs=(pl.BlockSpec(memory_space=pl.ANY),) * 3,
            scratch_shapes=[dma((3,))],
            compiler_params=pltpu.CompilerParams(vmem_limit_bytes=2**20),
            name="put_out",
        )(*held)

    placed = (
        P("blk", "uly"),
        P("blk", "uly"),
        P("blk", "uly"),
        P("blk", "uly"),
        P(("blk", "uly"), None),
        P("uly", "blk"),
    )
    return jax.shard_map(
        body,
        mesh=mesh,
        in_specs=placed,
        out_specs=(P(("blk", "uly"), None), P(("blk", "uly"), None), P(("blk", "uly"), None)),
        check_vma=False,
    )
```

```python
import jax
import jax.numpy as jnp
from jax import lax
from jax.experimental import pallas as pl
from jax.experimental.pallas import tpu as pltpu
from jax.sharding import PartitionSpec as P

QHEADS = 40
KVHEADS = 8
HEAD_DIM = 128
STEPS = 3
MESH = pl.DeviceIdType.MESH
F32 = jnp.float32
BF16 = jnp.bfloat16

HOPS = ((2, 0), (2, 1), (1, 0), (3, 0), (1, 1), (3, 1), (0, 1))
INVERSE = (0, 1, 3, 2, 5, 4, 6)
FIRST = (0, 1, 2, 4, 3, 5, 6)
LAST = (6, 2, 4, 0, 1, 3, 5)


def dot_nt(a, b):
    return lax.dot_general(a, b, (((1,), (1,)), ((), ())), preferred_element_type=F32)


def dot_nn(a, b):
    return lax.dot_general(a, b, (((1,), (0,)), ((), ())), preferred_element_type=F32)


def kernel(
    blocks, ulys,
    q_hbm, k_hbm, v_hbm, o_hbm, g_hbm, lse_hbm,
    dq_out, dk_out, dv_out,
    q, k, v, o, g, lse, kt, prob, prob_low, dscore, delta, own, part, far, dq, final,
    local_sem, local_out_sem, g_send, g_recv, kv_send, kv_recv, p_send, p_recv,
    dq_send, dq_recv, f_send, f_recv, go_uly, go_blk,
):
    group = q.shape[1] // HEAD_DIM
    tokens = q.shape[0]
    piece = tokens // ulys
    width = q.shape[1]
    scale = HEAD_DIM ** -0.5
    b = lax.axis_index("blk")
    u = lax.axis_index("uly")
    chips = ulys // 2
    zc = u // 2
    core = u % 2

    def peer(hop):
        return ((zc + hop[0]) % chips) * 2 + (core + hop[1]) % 2

    peers = [peer(hop) for hop in HOPS]
    later = [(b + i) % blocks for i in range(STEPS)]
    earlier = [(b + blocks - i) % blocks for i in range(STEPS)]

    def zero(index, size):
        return 1 - (index + size - 1) // size

    def turn(to):
        return 2 * to + (ulys - 1) * zero(b, blocks) * zero(to, ulys)

    def place(block):
        return block % 3 + 3 * zero(block, blocks) * zero(u, ulys)

    now, mine = turn(u), place(b)
    others = [(turn(p), now) for p in peers] + [(place(x), mine) for x in later[1:] + earlier[1:]]
    before = sum((their < own_).astype(jnp.int32) for their, own_ in others)
    barrier = pltpu.get_barrier_semaphore()

    def tell(sem, index, to, when):
        @pl.when(when)
        def _():
            pl.semaphore_signal(sem if index is None else sem.at[index], inc=1, device_id=to, device_id_type=MESH)

    for n in FIRST:
        tell(barrier, None, (b, peers[n]), turn(peers[n]) > now)
    for i in range(1, STEPS):
        for other in (later[i], earlier[i]):
            tell(barrier, None, (other, u), place(other) > mine)

    def cols(index, size):
        return pl.ds(pl.multiple_of(index * size, size), size)

    locals_ = [
        pltpu.make_async_copy(q_hbm, q, local_sem.at[0]),
        pltpu.make_async_copy(k_hbm, k.at[0], local_sem.at[1]),
        pltpu.make_async_copy(lse_hbm, lse, local_sem.at[2]),
        pltpu.make_async_copy(v_hbm, v.at[0], local_sem.at[3]),
        pltpu.make_async_copy(o_hbm, o, local_sem.at[4]),
        pltpu.make_async_copy(g_hbm.at[:, cols(u, width)], g.at[cols(u, piece), :], local_sem.at[5]),
    ]
    for c in locals_:
        c.start()
    @pl.when(before > 0)
    def _():
        pl.semaphore_wait(barrier, before)

    for n in FIRST:
        tell(go_uly, INVERSE[n], (b, peers[n]), turn(peers[n]) < now)
    for i in range(1, STEPS):
        tell(go_blk, i - 1, (earlier[i], u), place(earlier[i]) < mine)
        tell(go_blk, STEPS - 2 + i, (later[i], u), place(later[i]) < mine)

    def await_go(sem, index, when):
        @pl.when(when)
        def _():
            pl.semaphore_wait(sem.at[index], 1)

    def remote(src, dst, send, recv, to):
        return pltpu.make_async_remote_copy(
            src_ref=src, dst_ref=dst, send_sem=send, recv_sem=recv, device_id=to, device_id_type=MESH
        )

    g_copies = [
        remote(g_hbm.at[:, cols(p, width)], g.at[cols(u, piece), :], g_send.at[n], g_recv.at[n], (b, p))
        for n, p in enumerate(peers)
    ]
    kv_copies = []
    for i in range(1, STEPS):
        kv_copies.append(remote(k_hbm, k.at[i], kv_send.at[0, i - 1], kv_recv.at[0, i - 1], (later[i], u)))
        kv_copies.append(remote(v_hbm, v.at[i], kv_send.at[1, i - 1], kv_recv.at[1, i - 1], (later[i], u)))
    def send_g(n, when):
        @pl.when(when)
        def _():
            g_copies[n].start()

    for i in range(1, STEPS):
        for c in kv_copies[2 * (i - 1) : 2 * i]:
            @pl.when(place(later[i]) < mine)
            def _():
                c.start()
    for n in FIRST:
        send_g(n, turn(peers[n]) < now)
    for i in range(1, STEPS):
        await_go(go_blk, i - 1, place(later[i]) > mine)
        for c in kv_copies[2 * (i - 1) : 2 * i]:
            @pl.when(place(later[i]) > mine)
            def _():
                c.start()
    for n in LAST:
        await_go(go_uly, n, turn(peers[n]) > now)
        send_g(n, turn(peers[n]) > now)

    def head(r):
        return slice(r * HEAD_DIM, (r + 1) * HEAD_DIM)

    for c in locals_[:3]:
        c.wait()
    for i in range(STEPS):
        if i:
            kv_copies[2 * (i - 1)].wait_recv()
        keys = k[i]
        kt[:, head(i)] = keys.T
        for r in range(group):
            s = dot_nt(keys, q[:, head(r)])
            p = jnp.exp(s * scale - lse[r : r + 1, :])
            prob[i, :, head(r)] = p
            prob_low[i, :, head(r)] = p.astype(BF16)

    for c in locals_[3:]:
        c.wait()
    for c in g_copies:
        c.wait_recv()

    grads = jnp.concatenate([g[:, head(r)] for r in range(group)], axis=0)
    queries = jnp.concatenate([q[:, head(r)] for r in range(group)], axis=0)
    part_copies = []

    def send_part(kind, i):
        c = remote(
            part.at[kind, i - 1], far.at[kind, i - 1], p_send.at[kind, i - 1], p_recv.at[kind, i - 1],
            (earlier[i], u),
        )
        c.start()
        part_copies.append(c)

    for i in range(1, STEPS):
        await_go(go_blk, STEPS - 2 + i, place(earlier[i]) > mine)
    for i in (2, 1, 0):
        dv = dot_nn(prob_low[i], grads)
        if i:
            part[1, i - 1] = dv.astype(BF16)
            send_part(1, i)
        else:
            own[1] = dv

    ones = jnp.ones((8, HEAD_DIM), BF16)
    for r in range(group):
        product = g[:, head(r)].astype(F32) * o[:, head(r)].astype(F32)
        high = product.astype(BF16)
        low = (product - high.astype(F32)).astype(BF16)
        delta[:, head(r)] = dot_nt(ones, high) + dot_nt(ones, low)

    for c in kv_copies[1::2]:
        c.wait_recv()
    for i in (2, 1, 0):
        for r in range(group):
            dp = dot_nt(v[i], g[:, head(r)])
            ds = prob[i, :, head(r)] * (dp - delta[0:1, head(r)])
            dscore[head(i), head(r)] = ds.astype(BF16)
        dk = dot_nn(dscore[head(i), :], queries)
        if i:
            part[0, i - 1] = dk.astype(BF16)
            send_part(0, i)
        else:
            own[0] = dk

    for r in range(group):
        dqt = dot_nn(kt[...], dscore[:, head(r)])
        dq[:, head(r)] = (dqt.T * scale).astype(BF16)

    dq_copies = []
    for n, p in enumerate(peers):
        c = remote(dq.at[cols(p, piece), :], dq_out.at[:, cols(u, width)], dq_send.at[n], dq_recv.at[n], (b, p))
        c.start()
        dq_copies.append(c)
    keep = [pltpu.make_async_copy(dq.at[cols(u, piece), :], dq_out.at[:, cols(u, width)], local_out_sem.at[0])]
    keep[0].start()

    final_copies = []
    for kind, out, factor in ((1, dv_out, None), (0, dk_out, scale)):
        for c in part_copies[2 * (1 - kind) : 2 * (2 - kind)]:
            c.wait_recv()
        total = own[kind] + far[kind, 0].astype(F32) + far[kind, 1].astype(F32)
        if factor is not None:
            total = total * factor
        final[kind] = total.astype(BF16)
        for n, p in enumerate(peers):
            c = remote(
                final.at[kind, cols(p, piece), :], out.at[:, cols(u, HEAD_DIM)],
                f_send.at[kind, n], f_recv.at[kind, n], (b, p),
            )
            c.start()
            final_copies.append(c)
        c = pltpu.make_async_copy(
            final.at[kind, cols(u, piece), :], out.at[:, cols(u, HEAD_DIM)], local_out_sem.at[1 + kind]
        )
        c.start()
        keep.append(c)

    for c in g_copies + kv_copies + part_copies:
        c.wait_send()
    for c in keep:
        c.wait()
    for c in dq_copies + final_copies:
        c.wait()


def put_out(a, b, c, a_out, b_out, c_out, sem):
    copies = [
        pltpu.make_async_copy(src, dst, sem.at[n])
        for n, (src, dst) in enumerate(((a, a_out), (b, b_out), (c, c_out)))
    ]
    for copy in copies:
        copy.start()
    for copy in copies:
        copy.wait()


def solution(mesh):
    blocks = mesh.shape["blk"]
    ulys = mesh.shape["uly"]

    def body(q, k, v, o, g, lse):
        tokens, width = q.shape
        group = width // HEAD_DIM
        piece = tokens // ulys
        peers = len(HOPS)
        far = STEPS - 1
        dma = pltpu.SemaphoreType.DMA
        held = pl.pallas_call(
            lambda *refs: kernel(blocks, ulys, *refs),
            out_shape=(
                pltpu.VMEM((piece, width * ulys), BF16),
                pltpu.VMEM((piece, HEAD_DIM * ulys), BF16),
                pltpu.VMEM((piece, HEAD_DIM * ulys), BF16),
            ),
            in_specs=[pl.BlockSpec(memory_space=pl.ANY)] * 6,
            out_specs=(pl.BlockSpec(memory_space=pl.ANY),) * 3,
            scratch_shapes=[
                pltpu.VMEM((tokens, width), BF16),
                pltpu.VMEM((STEPS, tokens, HEAD_DIM), BF16),
                pltpu.VMEM((STEPS, tokens, HEAD_DIM), BF16),
                pltpu.VMEM((tokens, width), BF16),
                pltpu.VMEM((tokens, width), BF16),
                pltpu.VMEM((group, tokens), F32),
                pltpu.VMEM((HEAD_DIM, STEPS * tokens), BF16),
                pltpu.VMEM((STEPS, tokens, width), F32),
                pltpu.VMEM((STEPS, tokens, width), BF16),
                pltpu.VMEM((STEPS * tokens, width), BF16),
                pltpu.VMEM((8, width), F32),
                pltpu.VMEM((2, tokens, HEAD_DIM), F32),
                pltpu.VMEM((2, far, tokens, HEAD_DIM), BF16),
                pltpu.VMEM((2, far, tokens, HEAD_DIM), BF16),
                pltpu.VMEM((tokens, width), BF16),
                pltpu.VMEM((2, tokens, HEAD_DIM), BF16),
                dma((6,)),
                dma((3,)),
                dma((peers,)),
                dma((peers,)),
                dma((2, far)),
                dma((2, far)),
                dma((2, far)),
                dma((2, far)),
                dma((peers,)),
                dma((peers,)),
                dma((2, peers)),
                dma((2, peers)),
                pltpu.SemaphoreType.REGULAR((peers,)),
                pltpu.SemaphoreType.REGULAR((2 * far,)),
            ],
            compiler_params=pltpu.CompilerParams(collective_id=0, has_side_effects=True),
            name="grads",
        )(q, k, v, o, g, lse)
        return pl.pallas_call(
            put_out,
            out_shape=tuple(jax.ShapeDtypeStruct(x.shape, x.dtype) for x in held),
            in_specs=[pl.BlockSpec(memory_space=pl.ANY)] * 3,
            out_specs=(pl.BlockSpec(memory_space=pl.ANY),) * 3,
            scratch_shapes=[dma((3,))],
            compiler_params=pltpu.CompilerParams(vmem_limit_bytes=2**20),
            name="put_out",
        )(*held)

    placed = (
        P("blk", "uly"),
        P("blk", "uly"),
        P("blk", "uly"),
        P("blk", "uly"),
        P(("blk", "uly"), None),
        P("uly", "blk"),
    )
    return jax.shard_map(
        body,
        mesh=mesh,
        in_specs=placed,
        out_specs=(P(("blk", "uly"), None), P(("blk", "uly"), None), P(("blk", "uly"), None)),
        check_vma=False,
    )
```

```python
import jax
import jax.numpy as jnp
from jax import lax
from jax.experimental import pallas as pl
from jax.experimental.pallas import tpu as pltpu
from jax.sharding import PartitionSpec as P

QHEADS = 40
KVHEADS = 8
HEAD_DIM = 128
STEPS = 3
MESH = pl.DeviceIdType.MESH
F32 = jnp.float32
BF16 = jnp.bfloat16

HOPS = ((2, 0), (2, 1), (1, 0), (3, 0), (1, 1), (3, 1), (0, 1))
INVERSE = (0, 1, 3, 2, 5, 4, 6)
SOONER = (0,)
FINALS = (0, 1, 2, 3)
FIRST = (0, 1, 2, 4, 3, 5, 6)
NEAR = (5, 6, 0, 1, 2, 3, 4)
LAST = (2, 4, 0, 1, 3, 5, 6)


def dot_nt(a, b):
    return lax.dot_general(a, b, (((1,), (1,)), ((), ())), preferred_element_type=F32)


def dot_nn(a, b):
    return lax.dot_general(a, b, (((1,), (0,)), ((), ())), preferred_element_type=F32)


def kernel(
    blocks, ulys,
    q_hbm, k_hbm, v_hbm, o_hbm, g_hbm, lse_hbm,
    dq_out, dk_out, dv_out,
    q, k, v, o, g, lse, kt, prob, prob_low, dscore, delta, own, part, far, dq, final,
    local_sem, local_out_sem, g_send, g_recv, kv_send, kv_recv, p_send, p_recv,
    dq_send, dq_recv, f_send, f_recv, go_uly, go_blk, g_all,
):
    group = q.shape[1] // HEAD_DIM
    tokens = q.shape[0]
    piece = tokens // ulys
    width = q.shape[1]
    scale = HEAD_DIM ** -0.5
    b = lax.axis_index("blk")
    u = lax.axis_index("uly")
    chips = ulys // 2
    zc = u // 2
    core = u % 2

    def peer(hop):
        return ((zc + hop[0]) % chips) * 2 + (core + hop[1]) % 2

    peers = [peer(hop) for hop in HOPS]
    later = [(b + i) % blocks for i in range(STEPS)]
    earlier = [(b + blocks - i) % blocks for i in range(STEPS)]

    def zero(index, size):
        return 1 - (index + size - 1) // size

    def turn(to):
        return 2 * to + (ulys - 1) * zero(b, blocks) * zero(to, ulys)

    def place(block):
        return block % 3 + 3 * zero(block, blocks) * zero(u, ulys)

    now, mine = turn(u), place(b)
    others = [(turn(p), now) for p in peers] + [(place(x), mine) for x in later[1:] + earlier[1:]]
    before = sum((their < own_).astype(jnp.int32) for their, own_ in others)
    barrier = pltpu.get_barrier_semaphore()

    def tell(sem, index, to, when):
        @pl.when(when)
        def _():
            pl.semaphore_signal(sem if index is None else sem.at[index], inc=1, device_id=to, device_id_type=MESH)

    for n in FIRST:
        tell(barrier, None, (b, peers[n]), turn(peers[n]) > now)
    for i in range(1, STEPS):
        for other in (later[i], earlier[i]):
            tell(barrier, None, (other, u), place(other) > mine)

    def cols(index, size):
        return pl.ds(pl.multiple_of(index * size, size), size)

    locals_ = [
        pltpu.make_async_copy(q_hbm, q, local_sem.at[0]),
        pltpu.make_async_copy(k_hbm, k.at[0], local_sem.at[1]),
        pltpu.make_async_copy(lse_hbm, lse, local_sem.at[2]),
        pltpu.make_async_copy(v_hbm, v.at[0], local_sem.at[3]),
        pltpu.make_async_copy(o_hbm, o, local_sem.at[4]),
        pltpu.make_async_copy(g_hbm.at[:, cols(u, width)], g.at[cols(u, piece), :], local_sem.at[5]),
    ]
    slab = pltpu.make_async_copy(g_hbm, g_all, local_sem.at[6])
    slab.start()
    for c in locals_:
        c.start()
    @pl.when(before > 0)
    def _():
        pl.semaphore_wait(barrier, before)

    for n in FIRST:
        tell(go_uly, INVERSE[n], (b, peers[n]), turn(peers[n]) < now)
    for i in range(1, STEPS):
        tell(go_blk, i - 1, (earlier[i], u), place(earlier[i]) < mine)
        tell(go_blk, STEPS - 2 + i, (later[i], u), place(later[i]) < mine)

    def await_go(sem, index, when):
        @pl.when(when)
        def _():
            pl.semaphore_wait(sem.at[index], 1)

    def remote(src, dst, send, recv, to):
        return pltpu.make_async_remote_copy(
            src_ref=src, dst_ref=dst, send_sem=send, recv_sem=recv, device_id=to, device_id_type=MESH
        )

    g_copies = [
        remote(g_all.at[:, cols(p, width)], g.at[cols(u, piece), :], g_send.at[n], g_recv.at[n], (b, p))
        for n, p in enumerate(peers)
    ]
    kv_copies = []
    for i in range(1, STEPS):
        kv_copies.append(remote(k_hbm, k.at[i], kv_send.at[0, i - 1], kv_recv.at[0, i - 1], (later[i], u)))
        kv_copies.append(remote(v_hbm, v.at[i], kv_send.at[1, i - 1], kv_recv.at[1, i - 1], (later[i], u)))
    def send_g(n, when):
        @pl.when(when)
        def _():
            g_copies[n].start()

    for i in range(1, STEPS):
        for c in kv_copies[2 * (i - 1) : 2 * i]:
            @pl.when(place(later[i]) < mine)
            def _():
                c.start()
    slab.wait()
    for n in FIRST:
        send_g(n, turn(peers[n]) < now)
    for i in range(1, STEPS):
        await_go(go_blk, i - 1, place(later[i]) > mine)
        for c in kv_copies[2 * (i - 1) : 2 * i]:
            @pl.when(place(later[i]) > mine)
            def _():
                c.start()
    for n in LAST:
        await_go(go_uly, n, turn(peers[n]) > now)
        send_g(n, turn(peers[n]) > now)

    def head(r):
        return slice(r * HEAD_DIM, (r + 1) * HEAD_DIM)

    for c in locals_[:3]:
        c.wait()
    for i in range(STEPS):
        if i:
            kv_copies[2 * (i - 1)].wait_recv()
        keys = k[i]
        kt[:, head(i)] = keys.T
        for r in range(group):
            s = dot_nt(keys, q[:, head(r)])
            p = jnp.exp(s * scale - lse[r : r + 1, :])
            prob[i, :, head(r)] = p
            prob_low[i, :, head(r)] = p.astype(BF16)

    for c in locals_[3:]:
        c.wait()
    for c in g_copies:
        c.wait_recv()

    grads = jnp.concatenate([g[:, head(r)] for r in range(group)], axis=0)
    queries = jnp.concatenate([q[:, head(r)] for r in range(group)], axis=0)
    part_copies = []

    def send_part(kind, i):
        c = remote(
            part.at[kind, i - 1], far.at[kind, i - 1], p_send.at[kind, i - 1], p_recv.at[kind, i - 1],
            (earlier[i], u),
        )
        c.start()
        part_copies.append(c)

    for i in range(1, STEPS):
        await_go(go_blk, STEPS - 2 + i, place(earlier[i]) > mine)
    rows = STEPS * tokens
    dv = dot_nn(prob_low[...].reshape(rows, width), grads)
    for i in (2, 1):
        part[1, i - 1] = dv[head(i)].astype(BF16)
        send_part(1, i)
    own[1] = dv[head(0)]

    ones = jnp.ones((8, HEAD_DIM), BF16)
    for r in range(group):
        product = g[:, head(r)].astype(F32) * o[:, head(r)].astype(F32)
        high = product.astype(BF16)
        low = (product - high.astype(F32)).astype(BF16)
        delta[:, head(r)] = dot_nt(ones, high) + dot_nt(ones, low)

    for c in kv_copies[1::2]:
        c.wait_recv()
    values = v[...].reshape(rows, HEAD_DIM)
    for r in range(group):
        dp = dot_nt(values, g[:, head(r)])
        ds = prob[:, :, head(r)].reshape(rows, HEAD_DIM) * (dp - delta[0:1, head(r)])
        dscore[:, head(r)] = ds.astype(BF16)
    dk = dot_nn(dscore[...], queries)
    for i in (2, 1):
        part[0, i - 1] = dk[head(i)].astype(BF16)
        send_part(0, i)
    own[0] = dk[head(0)]

    for r in range(group):
        dqt = dot_nn(kt[...], dscore[:, head(r)])
        dq[:, head(r)] = (dqt * scale).astype(BF16).T

    dq_copies = [
        remote(dq.at[cols(p, piece), :], dq_out.at[:, cols(u, width)], dq_send.at[n], dq_recv.at[n], (b, p))
        for n, p in enumerate(peers)
    ]
    final_copies = [
        [
            remote(
                final.at[kind, cols(p, piece), :], out.at[:, cols(u, HEAD_DIM)],
                f_send.at[kind, n], f_recv.at[kind, n], (b, p),
            )
            for n, p in enumerate(peers)
        ]
        for kind, out in ((0, dk_out), (1, dv_out))
    ]

    def start_some(copies, chips_):
        for n, p in enumerate(peers):
            @pl.when(sum((p // 2 == chip).astype(jnp.int32) for chip in chips_) > 0)
            def _():
                copies[n].start()

    start_some(dq_copies, SOONER)
    keep = [pltpu.make_async_copy(dq.at[cols(u, piece), :], dq_out.at[:, cols(u, width)], local_out_sem.at[0])]
    keep[0].start()

    for kind, out, factor in ((1, dv_out, None), (0, dk_out, scale)):
        for c in part_copies[2 * (1 - kind) : 2 * (2 - kind)]:
            c.wait_recv()
        total = own[kind] + far[kind, 0].astype(F32) + far[kind, 1].astype(F32)
        if factor is not None:
            total = total * factor
        final[kind] = total.astype(BF16)
        start_some(final_copies[kind], FINALS)
        c = pltpu.make_async_copy(
            final.at[kind, cols(u, piece), :], out.at[:, cols(u, HEAD_DIM)], local_out_sem.at[1 + kind]
        )
        c.start()
        keep.append(c)
    for chip in range(chips):
        if chip not in SOONER:
            start_some(dq_copies, (chip,))
        if chip not in FINALS:
            start_some(final_copies[1], (chip,))
            start_some(final_copies[0], (chip,))
    final_copies = final_copies[0] + final_copies[1]

    for c in g_copies + kv_copies + part_copies:
        c.wait_send()
    for c in keep:
        c.wait()
    for c in dq_copies + final_copies:
        c.wait()


def put_out(a, b, c, a_out, b_out, c_out, sem):
    copies = [
        pltpu.make_async_copy(src, dst, sem.at[n])
        for n, (src, dst) in enumerate(((a, a_out), (b, b_out), (c, c_out)))
    ]
    for copy in copies:
        copy.start()
    for copy in copies:
        copy.wait()


def solution(mesh):
    blocks = mesh.shape["blk"]
    ulys = mesh.shape["uly"]

    def body(q, k, v, o, g, lse):
        tokens, width = q.shape
        group = width // HEAD_DIM
        piece = tokens // ulys
        peers = len(HOPS)
        far = STEPS - 1
        dma = pltpu.SemaphoreType.DMA
        held = pl.pallas_call(
            lambda *refs: kernel(blocks, ulys, *refs),
            out_shape=(
                pltpu.VMEM((piece, width * ulys), BF16),
                pltpu.VMEM((piece, HEAD_DIM * ulys), BF16),
                pltpu.VMEM((piece, HEAD_DIM * ulys), BF16),
            ),
            in_specs=[pl.BlockSpec(memory_space=pl.ANY)] * 6,
            out_specs=(pl.BlockSpec(memory_space=pl.ANY),) * 3,
            scratch_shapes=[
                pltpu.VMEM((tokens, width), BF16),
                pltpu.VMEM((STEPS, tokens, HEAD_DIM), BF16),
                pltpu.VMEM((STEPS, tokens, HEAD_DIM), BF16),
                pltpu.VMEM((tokens, width), BF16),
                pltpu.VMEM((tokens, width), BF16),
                pltpu.VMEM((group, tokens), F32),
                pltpu.VMEM((HEAD_DIM, STEPS * tokens), BF16),
                pltpu.VMEM((STEPS, tokens, width), F32),
                pltpu.VMEM((STEPS, tokens, width), BF16),
                pltpu.VMEM((STEPS * tokens, width), BF16),
                pltpu.VMEM((8, width), F32),
                pltpu.VMEM((2, tokens, HEAD_DIM), F32),
                pltpu.VMEM((2, far, tokens, HEAD_DIM), BF16),
                pltpu.VMEM((2, far, tokens, HEAD_DIM), BF16),
                pltpu.VMEM((tokens, width), BF16),
                pltpu.VMEM((2, tokens, HEAD_DIM), BF16),
                dma((7,)),
                dma((3,)),
                dma((peers,)),
                dma((peers,)),
                dma((2, far)),
                dma((2, far)),
                dma((2, far)),
                dma((2, far)),
                dma((peers,)),
                dma((peers,)),
                dma((2, peers)),
                dma((2, peers)),
                pltpu.SemaphoreType.REGULAR((peers,)),
                pltpu.SemaphoreType.REGULAR((2 * far,)),
                pltpu.VMEM((piece, width * ulys), BF16),
            ],
            compiler_params=pltpu.CompilerParams(collective_id=0, has_side_effects=True),
            name="grads",
        )(q, k, v, o, g, lse)
        return pl.pallas_call(
            put_out,
            out_shape=tuple(jax.ShapeDtypeStruct(x.shape, x.dtype) for x in held),
            in_specs=[pl.BlockSpec(memory_space=pl.ANY)] * 3,
            out_specs=(pl.BlockSpec(memory_space=pl.ANY),) * 3,
            scratch_shapes=[dma((3,))],
            compiler_params=pltpu.CompilerParams(vmem_limit_bytes=2**20),
            name="put_out",
        )(*held)

    placed = (
        P("blk", "uly"),
        P("blk", "uly"),
        P("blk", "uly"),
        P("blk", "uly"),
        P(("blk", "uly"), None),
        P("uly", "blk"),
    )
    return jax.shard_map(
        body,
        mesh=mesh,
        in_specs=placed,
        out_specs=(P(("blk", "uly"), None), P(("blk", "uly"), None), P(("blk", "uly"), None)),
        check_vma=False,
    )
```

```python
import jax
import jax.numpy as jnp
from jax import lax
from jax.experimental import pallas as pl
from jax.experimental.pallas import tpu as pltpu
from jax.sharding import PartitionSpec as P

QHEADS = 40
KVHEADS = 8
HEAD_DIM = 128
STEPS = 3
MESH = pl.DeviceIdType.MESH
F32 = jnp.float32
BF16 = jnp.bfloat16

HOPS = ((2, 0), (2, 1), (1, 0), (3, 0), (1, 1), (3, 1), (0, 1))
INVERSE = (0, 1, 3, 2, 5, 4, 6)
SOONER = (0,)
FINALS = (0, 1, 2, 3)
FIRST = (0, 1, 2, 4, 3, 5, 6)
NEAR = (5, 6, 0, 1, 2, 3, 4)
LAST = (6, 2, 4, 0, 1, 3, 5)


def dot_nt(a, b):
    return lax.dot_general(a, b, (((1,), (1,)), ((), ())), preferred_element_type=F32)


def dot_nn(a, b):
    return lax.dot_general(a, b, (((1,), (0,)), ((), ())), preferred_element_type=F32)


def kernel(
    blocks, ulys,
    q_hbm, k_hbm, v_hbm, o_hbm, g_hbm, lse_hbm,
    dq_out, dk_out, dv_out,
    q, k, v, o, g, lse, kt, prob, prob_low, dscore, delta, own, part, far, dq, final,
    local_sem, local_out_sem, g_send, g_recv, kv_send, kv_recv, p_send, p_recv,
    dq_send, dq_recv, f_send, f_recv, go_uly, go_blk, g_all,
):
    group = q.shape[1] // HEAD_DIM
    tokens = q.shape[0]
    piece = tokens // ulys
    width = q.shape[1]
    scale = HEAD_DIM ** -0.5
    b = lax.axis_index("blk")
    u = lax.axis_index("uly")
    chips = ulys // 2
    zc = u // 2
    core = u % 2

    def peer(hop):
        return ((zc + hop[0]) % chips) * 2 + (core + hop[1]) % 2

    peers = [peer(hop) for hop in HOPS]
    later = [(b + i) % blocks for i in range(STEPS)]
    earlier = [(b + blocks - i) % blocks for i in range(STEPS)]

    def zero(index, size):
        return 1 - (index + size - 1) // size

    def turn(to):
        return 2 * to + (ulys - 1) * zero(b, blocks) * zero(to, ulys)

    def place(block):
        return block % 3 + 3 * zero(block, blocks) * zero(u, ulys)

    now, mine = turn(u), place(b)
    others = [(turn(p), now) for p in peers] + [(place(x), mine) for x in later[1:] + earlier[1:]]
    before = sum((their < own_).astype(jnp.int32) for their, own_ in others)
    barrier = pltpu.get_barrier_semaphore()

    def tell(sem, index, to, when):
        @pl.when(when)
        def _():
            pl.semaphore_signal(sem if index is None else sem.at[index], inc=1, device_id=to, device_id_type=MESH)

    for n in FIRST:
        tell(barrier, None, (b, peers[n]), turn(peers[n]) > now)
    for i in range(1, STEPS):
        for other in (later[i], earlier[i]):
            tell(barrier, None, (other, u), place(other) > mine)

    def cols(index, size):
        return pl.ds(pl.multiple_of(index * size, size), size)

    locals_ = [
        pltpu.make_async_copy(q_hbm, q, local_sem.at[0]),
        pltpu.make_async_copy(k_hbm, k.at[0], local_sem.at[1]),
        pltpu.make_async_copy(lse_hbm, lse, local_sem.at[2]),
        pltpu.make_async_copy(v_hbm, v.at[0], local_sem.at[3]),
        pltpu.make_async_copy(o_hbm, o, local_sem.at[4]),
        pltpu.make_async_copy(g_hbm.at[:, cols(u, width)], g.at[cols(u, piece), :], local_sem.at[5]),
    ]
    slab = pltpu.make_async_copy(g_hbm, g_all, local_sem.at[6])
    slab.start()
    for c in locals_:
        c.start()
    @pl.when(before > 0)
    def _():
        pl.semaphore_wait(barrier, before)

    for n in FIRST:
        tell(go_uly, INVERSE[n], (b, peers[n]), turn(peers[n]) < now)
    for i in range(1, STEPS):
        tell(go_blk, i - 1, (earlier[i], u), place(earlier[i]) < mine)
        tell(go_blk, STEPS - 2 + i, (later[i], u), place(later[i]) < mine)

    def await_go(sem, index, when):
        @pl.when(when)
        def _():
            pl.semaphore_wait(sem.at[index], 1)

    def remote(src, dst, send, recv, to):
        return pltpu.make_async_remote_copy(
            src_ref=src, dst_ref=dst, send_sem=send, recv_sem=recv, device_id=to, device_id_type=MESH
        )

    g_copies = [
        remote(g_all.at[:, cols(p, width)], g.at[cols(u, piece), :], g_send.at[n], g_recv.at[n], (b, p))
        for n, p in enumerate(peers)
    ]
    kv_copies = []
    for i in range(1, STEPS):
        kv_copies.append(remote(k_hbm, k.at[i], kv_send.at[0, i - 1], kv_recv.at[0, i - 1], (later[i], u)))
        kv_copies.append(remote(v_hbm, v.at[i], kv_send.at[1, i - 1], kv_recv.at[1, i - 1], (later[i], u)))
    def send_g(n, when):
        @pl.when(when)
        def _():
            g_copies[n].start()

    for i in range(1, STEPS):
        for c in kv_copies[2 * (i - 1) : 2 * i]:
            @pl.when(place(later[i]) < mine)
            def _():
                c.start()
    slab.wait()
    for n in FIRST:
        send_g(n, turn(peers[n]) < now)
    for i in range(1, STEPS):
        await_go(go_blk, i - 1, place(later[i]) > mine)
        for c in kv_copies[2 * (i - 1) : 2 * i]:
            @pl.when(place(later[i]) > mine)
            def _():
                c.start()
    for n in LAST:
        await_go(go_uly, n, turn(peers[n]) > now)
        send_g(n, turn(peers[n]) > now)

    def head(r):
        return slice(r * HEAD_DIM, (r + 1) * HEAD_DIM)

    for c in locals_[:3]:
        c.wait()
    for i in range(STEPS):
        if i:
            kv_copies[2 * (i - 1)].wait_recv()
        keys = k[i]
        kt[:, head(i)] = keys.T
        for r in range(group):
            s = dot_nt(keys, q[:, head(r)])
            p = jnp.exp(s * scale - lse[r : r + 1, :])
            prob[i, :, head(r)] = p
            prob_low[i, :, head(r)] = p.astype(BF16)

    for c in locals_[3:]:
        c.wait()
    for c in g_copies:
        c.wait_recv()

    grads = jnp.concatenate([g[:, head(r)] for r in range(group)], axis=0)
    queries = jnp.concatenate([q[:, head(r)] for r in range(group)], axis=0)
    part_copies = []

    def send_part(kind, i):
        c = remote(
            part.at[kind, i - 1], far.at[kind, i - 1], p_send.at[kind, i - 1], p_recv.at[kind, i - 1],
            (earlier[i], u),
        )
        c.start()
        part_copies.append(c)

    for i in range(1, STEPS):
        await_go(go_blk, STEPS - 2 + i, place(earlier[i]) > mine)
    rows = STEPS * tokens
    dv = dot_nn(prob_low[...].reshape(rows, width), grads)
    for i in (2, 1):
        part[1, i - 1] = dv[head(i)].astype(BF16)
        send_part(1, i)
    own[1] = dv[head(0)]

    ones = jnp.ones((8, HEAD_DIM), BF16)
    for r in range(group):
        product = g[:, head(r)].astype(F32) * o[:, head(r)].astype(F32)
        high = product.astype(BF16)
        low = (product - high.astype(F32)).astype(BF16)
        delta[:, head(r)] = dot_nt(ones, high) + dot_nt(ones, low)

    for c in kv_copies[1::2]:
        c.wait_recv()
    values = v[...].reshape(rows, HEAD_DIM)
    for r in range(group):
        dp = dot_nt(values, g[:, head(r)])
        ds = prob[:, :, head(r)].reshape(rows, HEAD_DIM) * (dp - delta[0:1, head(r)])
        dscore[:, head(r)] = ds.astype(BF16)
    dk = dot_nn(dscore[...], queries)
    for i in (2, 1):
        part[0, i - 1] = dk[head(i)].astype(BF16)
        send_part(0, i)
    own[0] = dk[head(0)]

    for r in range(group):
        dqt = dot_nn(kt[...], dscore[:, head(r)])
        dq[:, head(r)] = (dqt * scale).astype(BF16).T

    dq_copies = [
        remote(dq.at[cols(p, piece), :], dq_out.at[:, cols(u, width)], dq_send.at[n], dq_recv.at[n], (b, p))
        for n, p in enumerate(peers)
    ]
    final_copies = [
        [
            remote(
                final.at[kind, cols(p, piece), :], out.at[:, cols(u, HEAD_DIM)],
                f_send.at[kind, n], f_recv.at[kind, n], (b, p),
            )
            for n, p in enumerate(peers)
        ]
        for kind, out in ((0, dk_out), (1, dv_out))
    ]

    def start_some(copies, chips_):
        for n, p in enumerate(peers):
            @pl.when(sum((p // 2 == chip).astype(jnp.int32) for chip in chips_) > 0)
            def _():
                copies[n].start()

    start_some(dq_copies, SOONER)
    keep = [pltpu.make_async_copy(dq.at[cols(u, piece), :], dq_out.at[:, cols(u, width)], local_out_sem.at[0])]
    keep[0].start()

    for kind, out, factor in ((1, dv_out, None), (0, dk_out, scale)):
        for c in part_copies[2 * (1 - kind) : 2 * (2 - kind)]:
            c.wait_recv()
        total = own[kind] + far[kind, 0].astype(F32) + far[kind, 1].astype(F32)
        if factor is not None:
            total = total * factor
        final[kind] = total.astype(BF16)
        start_some(final_copies[kind], FINALS)
        c = pltpu.make_async_copy(
            final.at[kind, cols(u, piece), :], out.at[:, cols(u, HEAD_DIM)], local_out_sem.at[1 + kind]
        )
        c.start()
        keep.append(c)
    for chip in range(chips):
        if chip not in SOONER:
            start_some(dq_copies, (chip,))
        if chip not in FINALS:
            start_some(final_copies[1], (chip,))
            start_some(final_copies[0], (chip,))
    final_copies = final_copies[0] + final_copies[1]

    for c in g_copies + kv_copies + part_copies:
        c.wait_send()
    for c in keep:
        c.wait()
    for c in dq_copies + final_copies:
        c.wait()


def put_out(a, b, c, a_out, b_out, c_out, sem):
    copies = [
        pltpu.make_async_copy(src, dst, sem.at[n])
        for n, (src, dst) in enumerate(((a, a_out), (b, b_out), (c, c_out)))
    ]
    for copy in copies:
        copy.start()
    for copy in copies:
        copy.wait()


def solution(mesh):
    blocks = mesh.shape["blk"]
    ulys = mesh.shape["uly"]

    def body(q, k, v, o, g, lse):
        tokens, width = q.shape
        group = width // HEAD_DIM
        piece = tokens // ulys
        peers = len(HOPS)
        far = STEPS - 1
        dma = pltpu.SemaphoreType.DMA
        held = pl.pallas_call(
            lambda *refs: kernel(blocks, ulys, *refs),
            out_shape=(
                pltpu.VMEM((piece, width * ulys), BF16),
                pltpu.VMEM((piece, HEAD_DIM * ulys), BF16),
                pltpu.VMEM((piece, HEAD_DIM * ulys), BF16),
            ),
            in_specs=[pl.BlockSpec(memory_space=pl.ANY)] * 6,
            out_specs=(pl.BlockSpec(memory_space=pl.ANY),) * 3,
            scratch_shapes=[
                pltpu.VMEM((tokens, width), BF16),
                pltpu.VMEM((STEPS, tokens, HEAD_DIM), BF16),
                pltpu.VMEM((STEPS, tokens, HEAD_DIM), BF16),
                pltpu.VMEM((tokens, width), BF16),
                pltpu.VMEM((tokens, width), BF16),
                pltpu.VMEM((group, tokens), F32),
                pltpu.VMEM((HEAD_DIM, STEPS * tokens), BF16),
                pltpu.VMEM((STEPS, tokens, width), F32),
                pltpu.VMEM((STEPS, tokens, width), BF16),
                pltpu.VMEM((STEPS * tokens, width), BF16),
                pltpu.VMEM((8, width), F32),
                pltpu.VMEM((2, tokens, HEAD_DIM), F32),
                pltpu.VMEM((2, far, tokens, HEAD_DIM), BF16),
                pltpu.VMEM((2, far, tokens, HEAD_DIM), BF16),
                pltpu.VMEM((tokens, width), BF16),
                pltpu.VMEM((2, tokens, HEAD_DIM), BF16),
                dma((7,)),
                dma((3,)),
                dma((peers,)),
                dma((peers,)),
                dma((2, far)),
                dma((2, far)),
                dma((2, far)),
                dma((2, far)),
                dma((peers,)),
                dma((peers,)),
                dma((2, peers)),
                dma((2, peers)),
                pltpu.SemaphoreType.REGULAR((peers,)),
                pltpu.SemaphoreType.REGULAR((2 * far,)),
                pltpu.VMEM((piece, width * ulys), BF16),
            ],
            compiler_params=pltpu.CompilerParams(collective_id=0, has_side_effects=True),
            name="grads",
        )(q, k, v, o, g, lse)
        return pl.pallas_call(
            put_out,
            out_shape=tuple(jax.ShapeDtypeStruct(x.shape, x.dtype) for x in held),
            in_specs=[pl.BlockSpec(memory_space=pl.ANY)] * 3,
            out_specs=(pl.BlockSpec(memory_space=pl.ANY),) * 3,
            scratch_shapes=[dma((3,))],
            compiler_params=pltpu.CompilerParams(vmem_limit_bytes=2**20),
            name="put_out",
        )(*held)

    placed = (
        P("blk", "uly"),
        P("blk", "uly"),
        P("blk", "uly"),
        P("blk", "uly"),
        P(("blk", "uly"), None),
        P("uly", "blk"),
    )
    return jax.shard_map(
        body,
        mesh=mesh,
        in_specs=placed,
        out_specs=(P(("blk", "uly"), None), P(("blk", "uly"), None), P(("blk", "uly"), None)),
        check_vma=False,
    )
```
